256 devices in a mesh: band: 32 (over x, z_hi, y), mem: 8 (over z_lo, core).
Axes of the slice: x: 4, y: 4, z: 8 (z_hi: 2, z_lo: 4; z = z_hi * 4 + z_lo), core: 2. Of those that a mesh axis runs over, the one named last changes fastest.
Arguments:
- state: float32 [32768, 8192], P('band', 'mem'), may hold values from -10 to 10
- obs_anom: bfloat16 [8192, 8192], P('band', 'mem'), may hold values from -8 to 8
- innov: float32 [8192, 8192], P('band', 'mem'), may hold values from -12 to 12
- pattern: int32 [32, 4, 8, 4], P('band'), may hold values 0 or 1
- distance: int32 [32, 4, 8, 4], P('band'), may hold values from 0 to 7
- taper: float32 [8], replicated, may hold values from 0.2 to 1
- order: int32 [32, 4], P('band'), may hold values from 0 to 3, each once within a row
Outputs:
- analysis: float32 [32768, 8192], P('band', 'mem')
The draws below stay inside these ranges and needn't reach their ends.
Inputs may be any that keep to these rules, and one draw needn't show every extreme that they name: Each row of order lists 0 .. 3 once each.
All inputs are finite; a program needn't handle non-finite values. No bound on the sum of `pattern` on one device may be relied on, other than what follows from the above.
Results may differ from the reference program's by a relative error of at most 0.0028.
Values may be sent and summed in bfloat16 or wider, within the bound.
No kernel may reach another device: no remote copies, remote signals or barrier semaphores. Data moves between devices by JAX's collectives and lax.ppermute only.
A program may use at most 64 MiB of HBM per device.

```python
import jax
import jax.numpy as jnp
from jax import lax

SB = 1024
OBS = 256
ARR = 4
DMAX = 8
RBLK = 8
OBLK = 4
BANDS = 32
MEMBERS = 8192
N_BAND = 32


def rough_values(seed_key, shape):
    return jax.random.normal(seed_key, shape, jnp.float32)


def latent_fields(key):
    latent_count = OBS // 4
    fields = rough_values(jax.random.fold_in(key, 7001), (BANDS, latent_count, MEMBERS))
    return fields


def band_rows(fields, seed_key, reach_bands, row_count, jitter_scale):
    latent_count = fields.shape[1]
    width = reach_bands * latent_count

    def one_band(band_index):
        picked = jnp.concatenate([lax.dynamic_index_in_dim(fields, (band_index - shift_by) % BANDS, 0, keepdims=False) for shift_by in range(reach_bands)], axis=0)
        band_key = jax.random.fold_in(seed_key, band_index)
        mixing = jax.random.normal(jax.random.fold_in(band_key, 1), (row_count, width), jnp.float32) / jnp.sqrt(jnp.float32(width))
        jitter = rough_values(jax.random.fold_in(band_key, 2), (row_count, fields.shape[2]))
        return jnp.dot(mixing, picked, precision=lax.Precision.HIGHEST) + jitter_scale * jitter
    return lax.map(one_band, jnp.arange(BANDS, dtype=jnp.int32))


def observed(key):
    fields = latent_fields(key)
    return band_rows(fields, jax.random.fold_in(key, 7200), 2, OBS, 0.4).reshape(BANDS * OBS, MEMBERS)


def draw_state(key, part):
    fields = latent_fields(key)
    values = band_rows(fields, jax.random.fold_in(key, 7100), 5, SB, 0.5).reshape(BANDS * SB, MEMBERS)
    return jnp.clip(values, -10.0, 10.0)


def draw_obs_anom(key, part):
    return jnp.clip(observed(key), -8.0, 8.0).astype(jnp.bfloat16)


def draw_innov(key, part):
    anomaly = observed(key)
    offset = rough_values(jax.random.fold_in(key, 7301), (BANDS * OBS, 1))
    perturb = rough_values(jax.random.fold_in(key, 7300), (BANDS * OBS, MEMBERS))
    return jnp.clip(offset - anomaly + perturb, -12.0, 12.0)


def set_ends(values, own_key, least, largest):
    shape = values.shape
    spot = [jax.random.randint(jax.random.fold_in(own_key, axis), (), 0, shape[axis]) for axis in range(len(shape))]
    values = values.at[tuple(spot)].set(least)
    longest = shape.index(max(shape))
    spot[longest] = (spot[longest] + 1) % shape[longest]
    return values.at[tuple(spot)].set(largest)


def setup_inputs(seed: int = 0) -> dict:
    arg_keys = jax.random.split(jax.random.key(seed), 8)
    state = draw_state(jax.random.fold_in(arg_keys[7], 71), 0)
    obs_anom = draw_obs_anom(jax.random.fold_in(arg_keys[7], 71), 0)
    innov = draw_innov(jax.random.fold_in(arg_keys[7], 71), 0)
    pattern = set_ends((jax.random.randint(arg_keys[3], (BANDS, ARR, RBLK, OBLK), 0, 4) < 3).astype(jnp.int32), jax.random.fold_in(arg_keys[3], 1), 0, 1)
    distance = set_ends(jax.random.randint(arg_keys[4], (BANDS, ARR, RBLK, OBLK), 0, DMAX), jax.random.fold_in(arg_keys[4], 1), 0, DMAX - 1).astype(jnp.int32)
    taper = jnp.clip(jax.random.uniform(arg_keys[5], (DMAX,), jnp.float32, 0.2, 1.0), 0.2, 1.0)
    order = jax.vmap(lambda own: jax.random.permutation(own, ARR))(jax.random.split(arg_keys[6], BANDS)).reshape((BANDS, ARR)).astype(jnp.int32)
    return {"state": state, "obs_anom": obs_anom, "innov": innov, "pattern": pattern, "distance": distance, "taper": taper, "order": order}


def spread(blocks):
    rows, cols = blocks.shape
    return jnp.broadcast_to(blocks[:, None, :, None], (rows, 128, cols, 64)).reshape(rows * 128, cols * 64)

def reference(state, obs_anom, innov, pattern, distance, taper, order):
    members = state.shape[1]
    scale = 1.0 / (members - 1)
    y_three = obs_anom.reshape(N_BAND, OBS, members)
    d_three = innov.reshape(N_BAND, OBS, members)

    def weigh(pair):
        y_batch, d_batch = pair
        gram = jnp.dot(y_batch.astype(jnp.float32), y_batch.T.astype(jnp.float32), preferred_element_type=jnp.float32)
        spd = gram * scale + jnp.eye(OBS, dtype=jnp.float32)
        factor = jnp.linalg.cholesky(spd)
        return jax.scipy.linalg.cho_solve((factor, True), d_batch).astype(jnp.bfloat16)
    w_three = lax.map(weigh, (y_three, d_three))
    onehot = (distance[..., None] == jnp.arange(DMAX, dtype=jnp.int32)).astype(jnp.float32)
    local = pattern.astype(jnp.float32) * jnp.sum(onehot * taper, axis=-1)
    x_three = state.reshape(N_BAND, SB, members)

    def band_update(index):
        field = lax.dynamic_index_in_dim(x_three, index, 0, keepdims=False)
        for step in range(ARR):
            offset = order[index, step]
            source = (index - offset) % N_BAND
            y_batch = y_three[source].astype(jnp.float32)
            w_batch = w_three[source].astype(jnp.float32)
            weights = spread(local[index, offset])
            cross = jnp.dot(field, y_batch.T, precision=lax.Precision.HIGHEST)
            field = field + jnp.dot(cross * scale * weights, w_batch, precision=lax.Precision.HIGHEST)
        return field
    result = lax.map(band_update, jnp.arange(N_BAND, dtype=jnp.int32))
    return result.reshape(state.shape)
```

```python
import jax
import jax.numpy as jnp
from jax import lax
from jax.experimental import pallas as pl
from jax.experimental.pallas import tpu as pltpu
from jax.sharding import PartitionSpec as P

HIGH = lax.Precision.HIGHEST
BF = jnp.bfloat16
F32 = jnp.float32
RING = 4


def mem_swap(value, bit):
    count = lax.axis_size("mem")
    return lax.ppermute(value, "mem", [(m, m ^ bit) for m in range(count)])


def band_send(value, pairs):
    return lax.ppermute(value, "band", pairs)


def fetch_batches(own):
    bands = lax.axis_size("band")
    y = lax.axis_index("band") % RING
    ahead = [
        band_send(own, [(s, s + r) for s in range(bands) if s % RING + r < RING])
        for r in range(1, RING)
    ]
    prev = band_send(own, [(s, (s + RING) % bands) for s in range(bands) if s % RING])
    wrapped = [
        band_send(prev, [(s, s + r - RING) for s in range(bands) if s % RING + r >= RING])
        for r in range(1, RING)
    ]
    return [jnp.where(y >= r, ahead[r - 1], wrapped[r - 1]) for r in range(1, RING)]


def dot(a, b, dims, precision=None):
    return lax.dot_general(a, b, (dims, ((), ())), precision=precision, preferred_element_type=F32)


def sum_scatter(part, z, core):
    keep = lax.dynamic_index_in_dim(part, core, 0, keepdims=False)
    give = lax.dynamic_index_in_dim(part, 1 - core, 0, keepdims=False)
    chip = keep + mem_swap(give.astype(BF), 1).astype(F32)
    total = lax.dynamic_index_in_dim(chip, z, 0, keepdims=False)
    chip16 = chip.astype(BF)
    for d in range(1, 4):
        block = lax.dynamic_index_in_dim(chip16, z ^ d, 0, keepdims=False)
        total = total + mem_swap(block, 2 * d).astype(F32)
    return total


def gather(block, z, core):
    line = jnp.stack([block] + [mem_swap(block, 2 * d) for d in range(1, 4)])
    half = jnp.stack([lax.dynamic_index_in_dim(line, z ^ k, 0, keepdims=False) for k in range(4)])
    other = mem_swap(half, 1)
    return jnp.where(core == 0, jnp.stack([half, other]), jnp.stack([other, half]))


def sum_all_f32(part, z, core):
    rows = part.shape[0] // 2
    halves = part.reshape(2, rows, part.shape[1])
    keep = lax.dynamic_index_in_dim(halves, core, 0, keepdims=False)
    give = lax.dynamic_index_in_dim(halves, 1 - core, 0, keepdims=False)
    half = keep + mem_swap(give, 1)
    total = half
    for d in range(1, 4):
        total = total + mem_swap(half, 2 * d)
    other = mem_swap(total, 1)
    return jnp.where(
        core == 0, jnp.concatenate([total, other]), jnp.concatenate([other, total])
    )


def weigh_kernel(scale, gram_ref, innov_ref, out_ref, x_ref, r_ref):
    n = gram_ref.shape[0]
    rows = lax.broadcasted_iota(jnp.int32, (n, n), 0)
    cols = lax.broadcasted_iota(jnp.int32, (n, n), 1)
    eye = jnp.where(rows == cols, 1.0, 0.0).astype(F32)
    a = gram_ref[...] * scale + eye
    most = jnp.max(jnp.sum(jnp.abs(a), axis=1, keepdims=True)) * 1.0001
    start = 2.0 / (1.0 + most)
    rho = (most - 1.0) / (most + 1.0)
    x_ref[...] = eye * start
    r_ref[...] = eye - a * start

    def unfinished(rho):
        return rho > 2e-3

    def improve(rho):
        square = rho * rho
        grow = 2.0 / (2.0 - square)
        x = x_ref[...]
        x = (x + jnp.dot(x, r_ref[...], precision=HIGH, preferred_element_type=F32)) * grow
        x_ref[...] = x
        r_ref[...] = eye - jnp.dot(a, x, precision=HIGH, preferred_element_type=F32)
        return square / (2.0 - square)

    lax.while_loop(unfinished, improve, rho)
    x = x_ref[...]
    x = x + jnp.dot(x, r_ref[...], precision=HIGH, preferred_element_type=F32)
    out_ref[...] = jnp.dot(
        x, innov_ref[...], precision=HIGH, preferred_element_type=F32
    ).astype(BF)


def weigh(gram, innov, scale):
    n, width = innov.shape
    return pl.pallas_call(
        lambda *refs: weigh_kernel(scale, *refs),
        out_shape=jax.ShapeDtypeStruct((n, width), BF),
        in_specs=[pl.BlockSpec(memory_space=pltpu.VMEM)] * 2,
        out_specs=pl.BlockSpec(memory_space=pltpu.VMEM),
        scratch_shapes=[pltpu.VMEM((n, n), F32)] * 2,
        name="weigh",
    )(gram, innov)


def on_device(state, obs_anom, innov, pattern, distance, taper, order):
    members = lax.axis_size("mem") * state.shape[1]
    scale = 1.0 / (members - 1)
    cells, width = state.shape
    num_obs = obs_anom.shape[0]
    arrivals = order.shape[1]
    mem = lax.axis_index("mem")
    z, core = mem // 2, mem % 2
    mine = core * 4 + z
    rows = cells // 8

    gram = sum_all_f32(dot(obs_anom, obs_anom, ((1,), (1,))), z, core)
    y_all = jnp.stack([obs_anom] + fetch_batches(obs_anom))
    weights = weigh(gram, innov, scale)
    w_all = jnp.stack([weights] + fetch_batches(weights))

    state16 = state.astype(BF)
    cross_part = jnp.concatenate(
        [dot(state16, y_all[a], ((1,), (1,))) for a in range(arrivals)], axis=1
    )
    cross = sum_scatter(cross_part.reshape(2, 4, rows, arrivals * num_obs), z, core)
    cross = cross.reshape(rows, arrivals, num_obs)

    first = [lax.dynamic_index_in_dim(w_all, order[0, t], 0, keepdims=False) for t in range(arrivals)]
    later = [lax.dynamic_index_in_dim(y_all, order[0, t], 0, keepdims=False) for t in range(arrivals)]
    pairs = [(t, s) for t in range(arrivals) for s in range(t + 1, arrivals)]
    link_part = jnp.concatenate(
        [dot(first[t], later[s], ((1,), (1,))) for t, s in pairs], axis=0
    )
    link_rows = link_part.shape[0] // 8
    link = gather(
        sum_scatter(link_part.reshape(2, 4, link_rows, num_obs), z, core).astype(BF), z, core
    ).reshape(len(pairs), num_obs, num_obs)

    onehot = (distance[0][..., None] == jnp.arange(taper.shape[0], dtype=jnp.int32)).astype(F32)
    local = pattern[0].astype(F32) * jnp.sum(onehot * taper, axis=-1)
    local = lax.dynamic_index_in_dim(local, mine, 1, keepdims=False) * scale
    span = num_obs // local.shape[1]
    coefs = []
    for s in range(arrivals):
        value = lax.dynamic_index_in_dim(cross, order[0, s], 1, keepdims=False)
        for t in range(s):
            value = value + dot(coefs[t], link[pairs.index((t, s))], ((1,), (0,)))
        factor = lax.dynamic_index_in_dim(local, order[0, s], 0, keepdims=False)
        factor = jnp.broadcast_to(factor[:, None], (factor.shape[0], span)).reshape(1, num_obs)
        coefs.append((value * factor).astype(BF))
    all_coefs = gather(jnp.concatenate(coefs, axis=1), z, core)
    w_cat = jnp.concatenate(first, axis=0)
    return state + dot(all_coefs.reshape(cells, arrivals * num_obs), w_cat, ((1,), (0,)))


def solution(mesh):
    return jax.shard_map(
        on_device,
        mesh=mesh,
        in_specs=(
            P("band", "mem"),
            P("band", "mem"),
            P("band", "mem"),
            P("band", None, None, None),
            P("band", None, None, None),
            P(),
            P("band", None),
        ),
        out_specs=P("band", "mem"),
        check_vma=False,
    )
```

```python
import jax
import jax.numpy as jnp
from jax import lax
from jax.experimental import pallas as pl
from jax.experimental.pallas import tpu as pltpu
from jax.sharding import PartitionSpec as P

HIGH = lax.Precision.HIGHEST
BF = jnp.bfloat16
F32 = jnp.float32
RING = 4
VMEM = pl.BlockSpec(memory_space=pltpu.VMEM)
SMEM = pl.BlockSpec(memory_space=pltpu.SMEM)
PARAMS = pltpu.CompilerParams(vmem_limit_bytes=48 * 2**20)


def shape(dims, dtype):
    return jax.ShapeDtypeStruct(dims, dtype)


def mem_swap(value, bit):
    count = lax.axis_size("mem")
    return lax.ppermute(value, "mem", [(m, m ^ bit) for m in range(count)])


def band_send(value, pairs):
    return lax.ppermute(value, "band", pairs)


def after(value, *deps):
    return lax.optimization_barrier((value,) + deps)[0]


def send_three(own):
    bands = lax.axis_size("band")
    return band_send(own, [(s, (s + 3) % bands) for s in range(bands)])


def send_ring(own):
    bands = lax.axis_size("band")
    one = band_send(own, [(s, s + 1) for s in range(bands) if s % RING < 3])
    two = band_send(own, [(s, s + 2) for s in range(bands) if s % RING < 2])
    return one, two


def wrap_batches(one, two, three):
    bands = lax.axis_size("band")
    y = lax.axis_index("band") % RING
    two_wrap = band_send(three, [(s, s - 1) for s in range(bands) if s % RING in (1, 2)])
    one_wrap = band_send(three, [(s, s - 2) for s in range(bands) if s % RING == 2])
    return jnp.where(y < 1, one_wrap, one), jnp.where(y < 2, two_wrap, two)


def dot_t(a, b):
    return lax.dot_general(a, b, (((1,), (1,)), ((), ())), preferred_element_type=F32)


def sum_gram(part, core, *gate):
    rows = part.shape[0] // 2
    halves = part.reshape(2, rows, part.shape[1])
    keep = lax.dynamic_index_in_dim(halves, core, 0, keepdims=False)
    give = lax.dynamic_index_in_dim(halves, 1 - core, 0, keepdims=False)
    half = keep + mem_swap(give, 1)
    half = half + after(mem_swap(half, 2), *gate)
    half = half + mem_swap(half, 4)
    return half, mem_swap(half, 1)


def split(x):
    top = x.astype(BF)
    return top, (x - top.astype(F32)).astype(BF)


def dot_split(a, b):
    (a_top, a_low), (b_top, b_low) = a, b
    small = jnp.dot(a_top, b_low, preferred_element_type=F32)
    small = small + jnp.dot(a_low, b_top, preferred_element_type=F32)
    return small + jnp.dot(a_top, b_top, preferred_element_type=F32)


def dot_high(a, b):
    return jnp.dot(a, b, precision=HIGH, preferred_element_type=F32)


def weigh_kernel(scale, ids_ref, half_ref, other_ref, innov_ref, out_ref, x_ref, a_ref):
    rows, n = half_ref.shape
    core = ids_ref[0]
    i = lax.broadcasted_iota(jnp.int32, (n, n), 0)
    j = lax.broadcasted_iota(jnp.int32, (n, n), 1)
    eye = jnp.where(i == j, 1.0, 0.0).astype(F32)
    a_ref[pl.ds(core * rows, rows), :] = half_ref[...] * scale
    a_ref[pl.ds((1 - core) * rows, rows), :] = other_ref[...] * scale
    a = a_ref[...] + eye
    a_ref[...] = a
    most = jnp.max(jnp.sum(jnp.abs(a), axis=1, keepdims=True)) * 1.0001
    rho = (most - 1.0) / (most + 1.0)
    square = rho * rho
    grow = 2.0 / (2.0 - square)
    start = 2.0 / (1.0 + most)
    x_ref[...] = (2.0 * eye - a * start) * (start * grow)
    rho = square / (2.0 - square)

    def improve(product, rho):
        square = rho * rho
        grow = 2.0 / (2.0 - square)
        x = x_ref[...]
        r = eye - product(a_ref[...], x)
        x_ref[...] = (x + product(x, r)) * grow
        return square / (2.0 - square)

    @pl.when(most < 200.0)
    def _():
        a_parts = split(a_ref[...])

        def improve_fast(rho):
            square = rho * rho
            grow = 2.0 / (2.0 - square)
            x = x_ref[...]
            r = eye - dot_split(a_parts, split(x))
            step = jnp.dot(x.astype(BF), r.astype(BF), preferred_element_type=F32)
            x_ref[...] = (x + step) * grow
            return square / (2.0 - square)

        lax.while_loop(lambda rho: rho > 5e-3, improve_fast, rho)

    @pl.when(most >= 200.0)
    def _():
        lax.while_loop(lambda rho: rho > 5e-3, lambda rho: improve(dot_high, rho), rho)

    x = x_ref[...]
    r = eye - dot_high(a_ref[...], x)
    x = x + jnp.dot(x.astype(BF), r.astype(BF), preferred_element_type=F32)
    out_ref[...] = dot_split(split(x), split(innov_ref[...])).astype(BF)


def weigh(ids, half, other, innov, scale):
    n, width = innov.shape
    return pl.pallas_call(
        lambda *refs: weigh_kernel(scale, *refs),
        out_shape=shape((n, width), BF),
        in_specs=[SMEM, VMEM, VMEM, VMEM],
        out_specs=VMEM,
        scratch_shapes=[pltpu.VMEM((n, n), F32)] * 2,
        compiler_params=PARAMS,
        name="weigh",
    )(ids, half, other, innov)


def cross_kernel(ids_ref, x_ref, y0_ref, y1_ref, y2_ref, y3_ref, give_ref, keep_ref):
    rows = give_ref.shape[1]
    core = ids_ref[0]
    x = x_ref[pl.ds((1 - core) * rows, rows), :].astype(BF)
    for a, y_ref in enumerate((y0_ref, y1_ref, y2_ref, y3_ref)):
        give_ref[a] = dot_t(x, y_ref[...]).astype(BF)
    x = x_ref[pl.ds(core * rows, rows), :].astype(BF)
    for a, y_ref in enumerate((y0_ref, y1_ref, y2_ref, y3_ref)):
        keep_ref[a] = dot_t(x, y_ref[...])


def cross_halves(ids, state, y):
    rows = state.shape[0] // 2
    num_obs = y[0].shape[0]
    return pl.pallas_call(
        cross_kernel,
        out_shape=[shape((4, rows, num_obs), BF), shape((4, rows, num_obs), F32)],
        in_specs=[SMEM] + [VMEM] * 5,
        out_specs=[VMEM, VMEM],
        compiler_params=PARAMS,
        name="cross",
    )(ids, state, *y)


def halve_kernel(bit, ids_ref, keep_ref, recv_ref, give_ref, out_ref):
    rows = give_ref.shape[1]
    own = pl.ds(ids_ref[bit] * rows, rows)
    far = pl.ds((1 - ids_ref[bit]) * rows, rows)
    give_ref[...] = (keep_ref[:, far, :] + recv_ref[:, far, :].astype(F32)).astype(BF)
    out_ref[...] = keep_ref[:, own, :] + recv_ref[:, own, :].astype(F32)


def halve(bit, ids, keep, recv):
    a, rows, cols = keep.shape
    dims = (a, rows // 2, cols)
    return pl.pallas_call(
        lambda *refs: halve_kernel(bit, *refs),
        out_shape=[shape(dims, BF), shape(dims, F32)],
        in_specs=[SMEM, VMEM, VMEM],
        out_specs=[VMEM, VMEM],
        compiler_params=PARAMS,
        name="halve",
    )(ids, keep, recv)


def link_kernel(pairs, ids_ref, order_ref, *refs):
    w_refs, y_refs, (give_ref, keep_ref, all_ref) = refs[:4], refs[4:8], refs[8:]
    n = all_ref.shape[2]
    for t in range(4):
        for s in range(4):
            if s != t:
                all_ref[4 * t + s] = dot_t(w_refs[t][...], y_refs[s][...])
    core = ids_ref[0]
    half = len(pairs) // 2

    def pick(p):
        first = second = 0
        for k, (t, s) in enumerate(pairs):
            first = jnp.where(p == k, order_ref[0, t], first)
            second = jnp.where(p == k, order_ref[0, s], second)
        return all_ref[4 * first + second]

    for k in range(half):
        give_ref[0, pl.ds(k * n, n), :] = pick((1 - core) * half + k).astype(BF)
        keep_ref[0, pl.ds(k * n, n), :] = pick(core * half + k)


def link_halves(ids, order, w, y, pairs):
    n = y[0].shape[0]
    dims = (1, len(pairs) // 2 * n, n)
    return pl.pallas_call(
        lambda *refs: link_kernel(pairs, *refs),
        out_shape=[shape(dims, BF), shape(dims, F32)],
        in_specs=[SMEM, SMEM] + [VMEM] * 8,
        out_specs=[VMEM, VMEM],
        scratch_shapes=[pltpu.VMEM((16, n, n), F32)],
        compiler_params=PARAMS,
        name="link",
    )(ids, order, *w, *y)


def solve_kernel(pairs, ids_ref, order_ref, keep_ref, recv_ref, link_ref, far_ref, local_ref, out_ref, all_ref):
    piece = link_ref.shape[2]
    n = local_ref.shape[2]
    mine = ids_ref[3]
    for k in range(4):
        all_ref[pl.ds((mine ^ k) * piece, piece), :] = link_ref[k, 0]
        all_ref[pl.ds((mine ^ (k + 4)) * piece, piece), :] = far_ref[k, 0]
    coefs = []
    for s in range(4):
        a = order_ref[0, s]
        value = keep_ref[a] + recv_ref[a].astype(F32)
        for t in range(s):
            block = all_ref[pl.ds(pairs.index((t, s)) * n, n), :]
            value = value + jnp.dot(coefs[t], block, preferred_element_type=F32)
        coefs.append((value * local_ref[a]).astype(BF))
        out_ref[a] = coefs[s]


def solve(ids, order, keep, recv, link, far, local, pairs):
    n = keep.shape[2]
    return pl.pallas_call(
        lambda *refs: solve_kernel(pairs, *refs),
        out_shape=shape(keep.shape, BF),
        in_specs=[SMEM, SMEM] + [VMEM] * 5,
        out_specs=VMEM,
        scratch_shapes=[pltpu.VMEM((len(pairs) * n, n), BF)],
        compiler_params=PARAMS,
        name="solve",
    )(ids, order, keep, recv, link, far, local)


def most_kernel(ids_ref, x_ref, *refs):
    near_refs, far_ref, w_refs, out_ref = refs[:3], refs[3], refs[4:8], refs[8]
    rows = far_ref.shape[2]
    mine = ids_ref[3]
    for part in range(2):
        total = 0.0
        for a, w_ref in enumerate(w_refs):
            blocks = [near_refs[k][a] if part == 0 else far_ref[k, a] for k in range(3)]
            left = jnp.concatenate(blocks, axis=0)
            total = total + jnp.dot(left, w_ref[...], preferred_element_type=F32)
        for k in range(3):
            spot = pl.ds((mine ^ (k + 4 * part)) * rows, rows)
            out_ref[spot, :] = x_ref[spot, :] + total[k * rows : (k + 1) * rows, :]


def update_most(ids, state, near, far, w):
    cells, width = state.shape
    n = w[0].shape[0]
    step = 256
    tall = pl.BlockSpec((cells, step), lambda i: (0, i))
    whole = pl.BlockSpec(near[0].shape, lambda i: (0, 0, 0))
    whole_far = pl.BlockSpec(far.shape, lambda i: (0, 0, 0, 0))
    return pl.pallas_call(
        most_kernel,
        out_shape=shape((cells, width), F32),
        grid=(width // step,),
        in_specs=[SMEM, tall] + [whole] * 3 + [whole_far]
        + [pl.BlockSpec((n, step), lambda i: (0, i))] * 4,
        out_specs=tall,
        compiler_params=PARAMS,
        name="update_most",
    )(ids, state, *near, far, *w)


def rest_kernel(ids_ref, x_ref, near_ref, far_ref, w0_ref, w1_ref, w2_ref, w3_ref, _, out_ref):
    first = pl.program_id(0) == 0
    total = x_ref[...]
    for a, w_ref in enumerate((w0_ref, w1_ref, w2_ref, w3_ref)):
        left = jnp.where(first, near_ref[a], far_ref[a])
        total = total + jnp.dot(left, w_ref[...], preferred_element_type=F32)
    out_ref[...] = total


def update_rest(ids, state, near, far, w, most):
    cells, width = state.shape
    n = w[0].shape[0]
    rows = near.shape[1]
    block = pl.BlockSpec((rows, width), lambda i, ids: (ids[3] ^ (3 + 4 * i), 0))
    coef = pl.BlockSpec(near.shape, lambda i, ids: (0, 0, 0))
    wide = pl.BlockSpec((n, width), lambda i, ids: (0, 0))
    return pl.pallas_call(
        rest_kernel,
        out_shape=shape((cells, width), F32),
        grid_spec=pltpu.PrefetchScalarGridSpec(
            num_scalar_prefetch=1,
            grid=(2,),
            in_specs=[block, coef, coef] + [wide] * 4 + [pl.BlockSpec(memory_space=pl.ANY)],
            out_specs=block,
        ),
        input_output_aliases={8: 0},
        compiler_params=PARAMS,
        name="update_rest",
    )(ids, state, near, far, *w, most)


def spread_up(block):
    pair = jnp.stack([block, mem_swap(block, 4)])
    near = jnp.concatenate([pair, mem_swap(pair, 2)])
    return near, mem_swap(near, 1)


def on_device(state, obs_anom, innov, pattern, distance, taper, order):
    members = lax.axis_size("mem") * state.shape[1]
    scale = 1.0 / (members - 1)
    num_obs = obs_anom.shape[0]
    arrivals = order.shape[1]
    mem = lax.axis_index("mem")
    core, low, high = mem % 2, mem // 2 % 2, mem // 4
    mine = core * 4 + low * 2 + high
    ids = jnp.stack([core, low, high, mine]).astype(jnp.int32)
    pairs = [(t, s) for t in range(arrivals) for s in range(t + 1, arrivals)]

    y_one, y_two = send_ring(obs_anom)
    y_three = send_three(obs_anom)
    half, other = sum_gram(dot_t(obs_anom, obs_anom), core, y_one, y_two, y_three)
    weights = weigh(ids, half, other, innov, scale)
    y = [obs_anom, *wrap_batches(y_one, y_two, y_three), y_three]
    w_three = send_three(weights)
    w_one, w_two = send_ring(after(weights, y[1], y[2]))
    give, keep = cross_halves(ids, state, y)
    w_three = after(w_three, w_one, w_two)
    w = [weights, *wrap_batches(w_one, w_two, w_three), w_three]
    give, keep = halve(1, ids, keep, after(mem_swap(after(give, w_three), 1)))
    give, keep = halve(2, ids, keep, mem_swap(give, 2))
    cross_recv = mem_swap(give, 4)

    link_give, link_keep = link_halves(ids, order, w, y, pairs)
    link_give, link_keep = halve(1, ids, link_keep, mem_swap(after(link_give, give), 1))
    link_recv = after(mem_swap(link_give, 2), cross_recv)
    link_give, link_keep = halve(2, ids, link_keep, link_recv)
    link = (link_keep + mem_swap(link_give, 4).astype(F32)).astype(BF)
    link_near, link_far = spread_up(link)

    onehot = (distance[0][..., None] == jnp.arange(taper.shape[0], dtype=jnp.int32)).astype(F32)
    local = pattern[0].astype(F32) * jnp.sum(onehot * taper, axis=-1)
    local = lax.dynamic_index_in_dim(local, mine, 1, keepdims=False) * scale
    local = jnp.repeat(local, num_obs // local.shape[1], axis=1)[:, None, :]
    coefs = solve(ids, order, keep, cross_recv, link_near, link_far, local, pairs)
    high_c = mem_swap(coefs, 4)
    low_c = mem_swap(coefs, 2)
    both_c = mem_swap(high_c, 2)
    far_most = mem_swap(jnp.stack([coefs, high_c, low_c]), 1)
    most = update_most(ids, state, [coefs, high_c, low_c], far_most, w)
    far_rest = mem_swap(after(both_c, most), 1)
    return update_rest(ids, state, both_c, far_rest, w, most)


def solution(mesh):
    return jax.shard_map(
        on_device,
        mesh=mesh,
        in_specs=(
            P("band", "mem"),
            P("band", "mem"),
            P("band", "mem"),
            P("band", None, None, None),
            P("band", None, None, None),
            P(),
            P("band", None),
        ),
        out_specs=P("band", "mem"),
        check_vma=False,
    )
```

```python
import jax
import jax.numpy as jnp
from jax import lax
from jax.experimental import pallas as pl
from jax.experimental.pallas import tpu as pltpu
from jax.sharding import PartitionSpec as P

HIGH = lax.Precision.HIGHEST
BF = jnp.bfloat16
F32 = jnp.float32
RING = 4
VMEM = pl.BlockSpec(memory_space=pltpu.VMEM)
SMEM = pl.BlockSpec(memory_space=pltpu.SMEM)
PARAMS = pltpu.CompilerParams(vmem_limit_bytes=48 * 2**20)


def shape(dims, dtype):
    return jax.ShapeDtypeStruct(dims, dtype)


def mem_swap(value, bit):
    count = lax.axis_size("mem")
    return lax.ppermute(value, "mem", [(m, m ^ bit) for m in range(count)])


def band_send(value, pairs):
    return lax.ppermute(value, "band", pairs)


def after(value, *deps):
    return lax.optimization_barrier((value,) + deps)[0]


def send_three(own):
    bands = lax.axis_size("band")
    return band_send(own, [(s, (s + 3) % bands) for s in range(bands)])


def send_one(own):
    bands = lax.axis_size("band")
    return band_send(own, [(s, s + 1) for s in range(bands) if s % RING < 3])


def send_two(one):
    bands = lax.axis_size("band")
    return band_send(one, [(s, s + 1) for s in range(bands) if s % RING in (1, 2)])


def wrap_batches(one, two, three):
    bands = lax.axis_size("band")
    y = lax.axis_index("band") % RING
    two_wrap = band_send(three, [(s, s - 1) for s in range(bands) if s % RING in (1, 2)])
    one_wrap = band_send(three, [(s, s - 2) for s in range(bands) if s % RING == 2])
    return jnp.where(y < 1, one_wrap, one), jnp.where(y < 2, two_wrap, two)


def dot_t(a, b):
    return lax.dot_general(a, b, (((1,), (1,)), ((), ())), preferred_element_type=F32)


def sum_gram(part, core):
    rows = part.shape[0] // 2
    halves = part.reshape(2, rows, part.shape[1])
    keep = lax.dynamic_index_in_dim(halves, core, 0, keepdims=False)
    give = lax.dynamic_index_in_dim(halves, 1 - core, 0, keepdims=False)
    half = keep + mem_swap(give, 1)
    half = half + mem_swap(half, 2)
    half = half + mem_swap(half, 4)
    return half, mem_swap(half, 1)


def split(x):
    top = x.astype(BF)
    return top, (x - top.astype(F32)).astype(BF)


def dot_split(a, b):
    (a_top, a_low), (b_top, b_low) = a, b
    small = jnp.dot(a_top, b_low, preferred_element_type=F32)
    small = small + jnp.dot(a_low, b_top, preferred_element_type=F32)
    return small + jnp.dot(a_top, b_top, preferred_element_type=F32)


def dot_high(a, b):
    return jnp.dot(a, b, precision=HIGH, preferred_element_type=F32)


def weigh_kernel(scale, ids_ref, half_ref, other_ref, innov_ref, out_ref, x_ref, a_ref):
    rows, n = half_ref.shape
    core = ids_ref[0]
    i = lax.broadcasted_iota(jnp.int32, (n, n), 0)
    j = lax.broadcasted_iota(jnp.int32, (n, n), 1)
    eye = jnp.where(i == j, 1.0, 0.0).astype(F32)
    a_ref[pl.ds(core * rows, rows), :] = half_ref[...] * scale
    a_ref[pl.ds((1 - core) * rows, rows), :] = other_ref[...] * scale
    a = a_ref[...] + eye
    a_ref[...] = a
    most = jnp.max(jnp.sum(jnp.abs(a), axis=1, keepdims=True)) * 1.0001
    rho = (most - 1.0) / (most + 1.0)
    square = rho * rho
    grow = 2.0 / (2.0 - square)
    start = 2.0 / (1.0 + most)
    x_ref[...] = (2.0 * eye - a * start) * (start * grow)
    rho = square / (2.0 - square)

    def improve(product, rho):
        square = rho * rho
        grow = 2.0 / (2.0 - square)
        x = x_ref[...]
        r = eye - product(a_ref[...], x)
        x_ref[...] = (x + product(x, r)) * grow
        return square / (2.0 - square)

    @pl.when(most < 200.0)
    def _():
        a_parts = split(a_ref[...])

        def improve_fast(rho):
            square = rho * rho
            grow = 2.0 / (2.0 - square)
            x = x_ref[...]
            r = eye - dot_split(a_parts, split(x))
            step = jnp.dot(x.astype(BF), r.astype(BF), preferred_element_type=F32)
            x_ref[...] = (x + step) * grow
            return square / (2.0 - square)

        lax.while_loop(lambda rho: rho > 5e-3, improve_fast, rho)

    @pl.when(most >= 200.0)
    def _():
        lax.while_loop(lambda rho: rho > 5e-3, lambda rho: improve(dot_high, rho), rho)

    x = x_ref[...]
    r = eye - dot_high(a_ref[...], x)
    x = x + jnp.dot(x.astype(BF), r.astype(BF), preferred_element_type=F32)
    out_ref[...] = dot_split(split(x), split(innov_ref[...])).astype(BF)


def weigh(ids, half, other, innov, scale):
    n, width = innov.shape
    return pl.pallas_call(
        lambda *refs: weigh_kernel(scale, *refs),
        out_shape=shape((n, width), BF),
        in_specs=[SMEM, VMEM, VMEM, VMEM],
        out_specs=VMEM,
        scratch_shapes=[pltpu.VMEM((n, n), F32)] * 2,
        compiler_params=PARAMS,
        name="weigh",
    )(ids, half, other, innov)


def cross_kernel(ids_ref, x_ref, y0_ref, y1_ref, y2_ref, y3_ref, give_ref, keep_ref):
    rows = give_ref.shape[1]
    core = ids_ref[0]
    x = x_ref[pl.ds((1 - core) * rows, rows), :].astype(BF)
    for a, y_ref in enumerate((y0_ref, y1_ref, y2_ref, y3_ref)):
        give_ref[a] = dot_t(x, y_ref[...]).astype(BF)
    x = x_ref[pl.ds(core * rows, rows), :].astype(BF)
    for a, y_ref in enumerate((y0_ref, y1_ref, y2_ref, y3_ref)):
        keep_ref[a] = dot_t(x, y_ref[...])


def cross_halves(ids, state, y):
    rows = state.shape[0] // 2
    num_obs = y[0].shape[0]
    return pl.pallas_call(
        cross_kernel,
        out_shape=[shape((4, rows, num_obs), BF), shape((4, rows, num_obs), F32)],
        in_specs=[SMEM] + [VMEM] * 5,
        out_specs=[VMEM, VMEM],
        compiler_params=PARAMS,
        name="cross",
    )(ids, state, *y)


def halve_kernel(bit, ids_ref, keep_ref, recv_ref, give_ref, out_ref):
    rows = give_ref.shape[1]
    own = pl.ds(ids_ref[bit] * rows, rows)
    far = pl.ds((1 - ids_ref[bit]) * rows, rows)
    give_ref[...] = (keep_ref[:, far, :] + recv_ref[:, far, :].astype(F32)).astype(BF)
    out_ref[...] = keep_ref[:, own, :] + recv_ref[:, own, :].astype(F32)


def halve(bit, ids, keep, recv):
    a, rows, cols = keep.shape
    dims = (a, rows // 2, cols)
    return pl.pallas_call(
        lambda *refs: halve_kernel(bit, *refs),
        out_shape=[shape(dims, BF), shape(dims, F32)],
        in_specs=[SMEM, VMEM, VMEM],
        out_specs=[VMEM, VMEM],
        compiler_params=PARAMS,
        name="halve",
    )(ids, keep, recv)


def link_kernel(pairs, ids_ref, order_ref, *refs):
    w_refs, y_refs, (give_ref, keep_ref, all_ref) = refs[:4], refs[4:8], refs[8:]
    n = all_ref.shape[2]
    for t in range(4):
        for s in range(4):
            if s != t:
                all_ref[4 * t + s] = dot_t(w_refs[t][...], y_refs[s][...])
    core = ids_ref[0]
    half = len(pairs) // 2

    def pick(p):
        first = second = 0
        for k, (t, s) in enumerate(pairs):
            first = jnp.where(p == k, order_ref[0, t], first)
            second = jnp.where(p == k, order_ref[0, s], second)
        return all_ref[4 * first + second]

    for k in range(half):
        give_ref[0, pl.ds(k * n, n), :] = pick((1 - core) * half + k).astype(BF)
        keep_ref[0, pl.ds(k * n, n), :] = pick(core * half + k)


def link_halves(ids, order, w, y, pairs):
    n = y[0].shape[0]
    dims = (1, len(pairs) // 2 * n, n)
    return pl.pallas_call(
        lambda *refs: link_kernel(pairs, *refs),
        out_shape=[shape(dims, BF), shape(dims, F32)],
        in_specs=[SMEM, SMEM] + [VMEM] * 8,
        out_specs=[VMEM, VMEM],
        scratch_shapes=[pltpu.VMEM((16, n, n), F32)],
        compiler_params=PARAMS,
        name="link",
    )(ids, order, *w, *y)


def solve_kernel(pairs, ids_ref, order_ref, keep_ref, recv_ref, link_ref, far_ref, local_ref, out_ref, all_ref):
    piece = link_ref.shape[2]
    n = local_ref.shape[2]
    mine = ids_ref[3]
    for k in range(4):
        all_ref[pl.ds((mine ^ k) * piece, piece), :] = link_ref[k, 0]
        all_ref[pl.ds((mine ^ (k + 4)) * piece, piece), :] = far_ref[k, 0]
    coefs = []
    for s in range(4):
        a = order_ref[0, s]
        value = keep_ref[a] + recv_ref[a].astype(F32)
        for t in range(s):
            block = all_ref[pl.ds(pairs.index((t, s)) * n, n), :]
            value = value + jnp.dot(coefs[t], block, preferred_element_type=F32)
        coefs.append((value * local_ref[a]).astype(BF))
        out_ref[a] = coefs[s]


def solve(ids, order, keep, recv, link, far, local, pairs):
    n = keep.shape[2]
    return pl.pallas_call(
        lambda *refs: solve_kernel(pairs, *refs),
        out_shape=shape(keep.shape, BF),
        in_specs=[SMEM, SMEM] + [VMEM] * 5,
        out_specs=VMEM,
        scratch_shapes=[pltpu.VMEM((len(pairs) * n, n), BF)],
        compiler_params=PARAMS,
        name="solve",
    )(ids, order, keep, recv, link, far, local)


def most_kernel(ids_ref, x_ref, *refs):
    near_refs, far_ref, w_refs, out_ref = refs[:3], refs[3], refs[4:8], refs[8]
    rows = far_ref.shape[2]
    mine = ids_ref[3]
    for part in range(2):
        total = 0.0
        for a, w_ref in enumerate(w_refs):
            blocks = [near_refs[k][a] if part == 0 else far_ref[k, a] for k in range(3)]
            left = jnp.concatenate(blocks, axis=0)
            total = total + jnp.dot(left, w_ref[...], preferred_element_type=F32)
        for k in range(3):
            spot = pl.ds((mine ^ (k + 4 * part)) * rows, rows)
            out_ref[spot, :] = x_ref[spot, :] + total[k * rows : (k + 1) * rows, :]


def update_most(ids, state, near, far, w):
    cells, width = state.shape
    n = w[0].shape[0]
    step = 256
    tall = pl.BlockSpec((cells, step), lambda i: (0, i))
    whole = pl.BlockSpec(near[0].shape, lambda i: (0, 0, 0))
    whole_far = pl.BlockSpec(far.shape, lambda i: (0, 0, 0, 0))
    return pl.pallas_call(
        most_kernel,
        out_shape=shape((cells, width), F32),
        grid=(width // step,),
        in_specs=[SMEM, tall] + [whole] * 3 + [whole_far]
        + [pl.BlockSpec((n, step), lambda i: (0, i))] * 4,
        out_specs=tall,
        compiler_params=PARAMS,
        name="update_most",
    )(ids, state, *near, far, *w)


def rest_kernel(ids_ref, x_ref, near_ref, far_ref, w0_ref, w1_ref, w2_ref, w3_ref, _, out_ref):
    first = pl.program_id(0) == 0
    total = x_ref[...]
    for a, w_ref in enumerate((w0_ref, w1_ref, w2_ref, w3_ref)):
        left = jnp.where(first, near_ref[a], far_ref[a])
        total = total + jnp.dot(left, w_ref[...], preferred_element_type=F32)
    out_ref[...] = total


def update_rest(ids, state, near, far, w, most):
    cells, width = state.shape
    n = w[0].shape[0]
    rows = near.shape[1]
    block = pl.BlockSpec((rows, width), lambda i, ids: (ids[3] ^ (3 + 4 * i), 0))
    coef = pl.BlockSpec(near.shape, lambda i, ids: (0, 0, 0))
    wide = pl.BlockSpec((n, width), lambda i, ids: (0, 0))
    return pl.pallas_call(
        rest_kernel,
        out_shape=shape((cells, width), F32),
        grid_spec=pltpu.PrefetchScalarGridSpec(
            num_scalar_prefetch=1,
            grid=(2,),
            in_specs=[block, coef, coef] + [wide] * 4 + [pl.BlockSpec(memory_space=pl.ANY)],
            out_specs=block,
        ),
        input_output_aliases={8: 0},
        compiler_params=PARAMS,
        name="update_rest",
    )(ids, state, near, far, *w, most)


def spread_up(block):
    pair = jnp.stack([block, mem_swap(block, 4)])
    near = jnp.concatenate([pair, mem_swap(pair, 2)])
    return near, mem_swap(near, 1)


def on_device(state, obs_anom, innov, pattern, distance, taper, order):
    members = lax.axis_size("mem") * state.shape[1]
    scale = 1.0 / (members - 1)
    num_obs = obs_anom.shape[0]
    arrivals = order.shape[1]
    mem = lax.axis_index("mem")
    core, low, high = mem % 2, mem // 2 % 2, mem // 4
    mine = core * 4 + low * 2 + high
    ids = jnp.stack([core, low, high, mine]).astype(jnp.int32)
    pairs = [(t, s) for t in range(arrivals) for s in range(t + 1, arrivals)]

    y_one = send_one(obs_anom)
    y_two = send_two(y_one)
    half, other = sum_gram(dot_t(obs_anom, obs_anom), core)
    y_three = send_three(after(obs_anom, half))
    weights = weigh(ids, half, other, innov, scale)
    w_three = send_three(weights)
    w_one = send_one(after(weights, y_one))
    w_two = send_two(after(w_one, y_two))
    y = [obs_anom, *wrap_batches(y_one, y_two, after(y_three, weights)), y_three]
    give, keep = cross_halves(ids, state, y)
    w_three = after(w_three, w_one, w_two)
    w = [weights, *wrap_batches(w_one, w_two, w_three), w_three]
    give, keep = halve(1, ids, keep, mem_swap(after(give, w_three), 1))
    give, keep = halve(2, ids, keep, mem_swap(give, 2))
    cross_recv = mem_swap(give, 4)

    link_give, link_keep = link_halves(ids, order, w, y, pairs)
    link_give, link_keep = halve(1, ids, link_keep, mem_swap(after(link_give, give), 1))
    link_recv = after(mem_swap(link_give, 2), cross_recv)
    link_give, link_keep = halve(2, ids, link_keep, link_recv)
    link = (link_keep + mem_swap(link_give, 4).astype(F32)).astype(BF)
    link_near, link_far = spread_up(link)

    onehot = (distance[0][..., None] == jnp.arange(taper.shape[0], dtype=jnp.int32)).astype(F32)
    local = pattern[0].astype(F32) * jnp.sum(onehot * taper, axis=-1)
    local = lax.dynamic_index_in_dim(local, mine, 1, keepdims=False) * scale
    local = jnp.repeat(local, num_obs // local.shape[1], axis=1)[:, None, :]
    coefs = solve(ids, order, keep, cross_recv, link_near, link_far, local, pairs)
    high_c = mem_swap(coefs, 4)
    low_c = mem_swap(coefs, 2)
    both_c = mem_swap(high_c, 2)
    far_most = mem_swap(jnp.stack([coefs, high_c, low_c]), 1)
    most = update_most(ids, state, [coefs, high_c, low_c], far_most, w)
    far_rest = mem_swap(after(both_c, most), 1)
    return update_rest(ids, state, both_c, far_rest, w, most)


def solution(mesh):
    return jax.shard_map(
        on_device,
        mesh=mesh,
        in_specs=(
            P("band", "mem"),
            P("band", "mem"),
            P("band", "mem"),
            P("band", None, None, None),
            P("band", None, None, None),
            P(),
            P("band", None),
        ),
        out_specs=P("band", "mem"),
        check_vma=False,
    )
```

```python
import jax
import jax.numpy as jnp
from jax import lax
from jax.experimental import pallas as pl
from jax.experimental.pallas import tpu as pltpu
from jax.sharding import PartitionSpec as P

HIGH = lax.Precision.HIGHEST
BF = jnp.bfloat16
F32 = jnp.float32
RING = 4
VMEM = pl.BlockSpec(memory_space=pltpu.VMEM)
SMEM = pl.BlockSpec(memory_space=pltpu.SMEM)
PARAMS = pltpu.CompilerParams(vmem_limit_bytes=48 * 2**20)


def shape(dims, dtype):
    return jax.ShapeDtypeStruct(dims, dtype)


def mem_swap(value, bit):
    count = lax.axis_size("mem")
    return lax.ppermute(value, "mem", [(m, m ^ bit) for m in range(count)])


def band_send(value, pairs):
    return lax.ppermute(value, "band", pairs)


def after(value, *deps):
    return lax.optimization_barrier((value,) + deps)[0]


def send_three(own):
    bands = lax.axis_size("band")
    return band_send(own, [(s, (s + 3) % bands) for s in range(bands)])


def send_one(own):
    bands = lax.axis_size("band")
    return band_send(own, [(s, s + 1) for s in range(bands) if s % RING < 3])


def send_two(one):
    bands = lax.axis_size("band")
    return band_send(one, [(s, s + 1) for s in range(bands) if s % RING in (1, 2)])


def send_wraps(three):
    bands = lax.axis_size("band")
    two = band_send(three, [(s, s - 1) for s in range(bands) if s % RING in (1, 2)])
    one = band_send(three, [(s, s - 2) for s in range(bands) if s % RING == 2])
    return one, two


def pick_batches(one, two, one_wrap, two_wrap):
    y = lax.axis_index("band") % RING
    return [jnp.where(y < 1, one_wrap, one), jnp.where(y < 2, two_wrap, two)]


def dot_t(a, b):
    return lax.dot_general(a, b, (((1,), (1,)), ((), ())), preferred_element_type=F32)


def sum_gram(part, core):
    rows = part.shape[0] // 2
    halves = part.reshape(2, rows, part.shape[1])
    keep = lax.dynamic_index_in_dim(halves, core, 0, keepdims=False)
    give = lax.dynamic_index_in_dim(halves, 1 - core, 0, keepdims=False)
    half = keep + mem_swap(give, 1)
    half = half + mem_swap(half, 2)
    half = half + mem_swap(half, 4)
    return half, mem_swap(half, 1)


def split(x):
    top = x.astype(BF)
    return top, (x - top.astype(F32)).astype(BF)


def dot_split(a, b):
    (a_top, a_low), (b_top, b_low) = a, b
    small = jnp.dot(a_top, b_low, preferred_element_type=F32)
    small = small + jnp.dot(a_low, b_top, preferred_element_type=F32)
    return small + jnp.dot(a_top, b_top, preferred_element_type=F32)


def dot_high(a, b):
    return jnp.dot(a, b, precision=HIGH, preferred_element_type=F32)


def weigh_kernel(scale, ids_ref, half_ref, other_ref, innov_ref, out_ref, x_ref, a_ref):
    rows, n = half_ref.shape
    core = ids_ref[0]
    i = lax.broadcasted_iota(jnp.int32, (n, n), 0)
    j = lax.broadcasted_iota(jnp.int32, (n, n), 1)
    eye = jnp.where(i == j, 1.0, 0.0).astype(F32)
    a_ref[pl.ds(core * rows, rows), :] = half_ref[...] * scale
    a_ref[pl.ds((1 - core) * rows, rows), :] = other_ref[...] * scale
    a = a_ref[...] + eye
    a_ref[...] = a
    most = jnp.max(jnp.sum(jnp.abs(a), axis=1, keepdims=True)) * 1.0001
    rho = (most - 1.0) / (most + 1.0)
    square = rho * rho
    grow = 2.0 / (2.0 - square)
    start = 2.0 / (1.0 + most)
    x_ref[...] = (2.0 * eye - a * start) * (start * grow)
    rho = square / (2.0 - square)

    def improve(product, rho):
        square = rho * rho
        grow = 2.0 / (2.0 - square)
        x = x_ref[...]
        r = eye - product(a_ref[...], x)
        x_ref[...] = (x + product(x, r)) * grow
        return square / (2.0 - square)

    @pl.when(most < 200.0)
    def _():
        a_parts = split(a_ref[...])

        def improve_fast(rho):
            square = rho * rho
            grow = 2.0 / (2.0 - square)
            x = x_ref[...]
            r = eye - dot_split(a_parts, split(x))
            step = jnp.dot(x.astype(BF), r.astype(BF), preferred_element_type=F32)
            x_ref[...] = (x + step) * grow
            return square / (2.0 - square)

        lax.while_loop(lambda rho: rho > 5e-3, improve_fast, rho)

    @pl.when(most >= 200.0)
    def _():
        lax.while_loop(lambda rho: rho > 5e-3, lambda rho: improve(dot_high, rho), rho)

    x = x_ref[...]
    r = eye - dot_high(a_ref[...], x)
    x = x + jnp.dot(x.astype(BF), r.astype(BF), preferred_element_type=F32)
    out_ref[...] = dot_split(split(x), split(innov_ref[...])).astype(BF)


def weigh(ids, half, other, innov, scale):
    n, width = innov.shape
    return pl.pallas_call(
        lambda *refs: weigh_kernel(scale, *refs),
        out_shape=shape((n, width), BF),
        in_specs=[SMEM, VMEM, VMEM, VMEM],
        out_specs=VMEM,
        scratch_shapes=[pltpu.VMEM((n, n), F32)] * 2,
        compiler_params=PARAMS,
        name="weigh",
    )(ids, half, other, innov)


def cross_kernel(ids_ref, x_ref, y0_ref, y1_ref, y2_ref, y3_ref, give_ref, keep_ref):
    rows = give_ref.shape[1]
    core = ids_ref[0]
    x = x_ref[pl.ds((1 - core) * rows, rows), :].astype(BF)
    for a, y_ref in enumerate((y0_ref, y1_ref, y2_ref, y3_ref)):
        give_ref[a] = dot_t(x, y_ref[...]).astype(BF)
    x = x_ref[pl.ds(core * rows, rows), :].astype(BF)
    for a, y_ref in enumerate((y0_ref, y1_ref, y2_ref, y3_ref)):
        keep_ref[a] = dot_t(x, y_ref[...])


def cross_halves(ids, state, y):
    rows = state.shape[0] // 2
    num_obs = y[0].shape[0]
    return pl.pallas_call(
        cross_kernel,
        out_shape=[shape((4, rows, num_obs), BF), shape((4, rows, num_obs), F32)],
        in_specs=[SMEM] + [VMEM] * 5,
        out_specs=[VMEM, VMEM],
        compiler_params=PARAMS,
        name="cross",
    )(ids, state, *y)


def halve_kernel(bit, ids_ref, keep_ref, recv_ref, give_ref, out_ref):
    rows = give_ref.shape[1]
    own = pl.ds(ids_ref[bit] * rows, rows)
    far = pl.ds((1 - ids_ref[bit]) * rows, rows)
    give_ref[...] = (keep_ref[:, far, :] + recv_ref[:, far, :].astype(F32)).astype(BF)
    out_ref[...] = keep_ref[:, own, :] + recv_ref[:, own, :].astype(F32)


def halve(bit, ids, keep, recv):
    a, rows, cols = keep.shape
    dims = (a, rows // 2, cols)
    return pl.pallas_call(
        lambda *refs: halve_kernel(bit, *refs),
        out_shape=[shape(dims, BF), shape(dims, F32)],
        in_specs=[SMEM, VMEM, VMEM],
        out_specs=[VMEM, VMEM],
        compiler_params=PARAMS,
        name="halve",
    )(ids, keep, recv)


def link_kernel(pairs, ids_ref, order_ref, *refs):
    w_refs, y_refs, (give_ref, keep_ref, all_ref) = refs[:4], refs[4:8], refs[8:]
    n = all_ref.shape[2]
    for t in range(4):
        for s in range(4):
            if s != t:
                all_ref[4 * t + s] = dot_t(w_refs[t][...], y_refs[s][...])
    core = ids_ref[0]
    half = len(pairs) // 2

    def pick(p):
        first = second = 0
        for k, (t, s) in enumerate(pairs):
            first = jnp.where(p == k, order_ref[0, t], first)
            second = jnp.where(p == k, order_ref[0, s], second)
        return all_ref[4 * first + second]

    for k in range(half):
        give_ref[0, pl.ds(k * n, n), :] = pick((1 - core) * half + k).astype(BF)
        keep_ref[0, pl.ds(k * n, n), :] = pick(core * half + k)


def link_halves(ids, order, w, y, pairs):
    n = y[0].shape[0]
    dims = (1, len(pairs) // 2 * n, n)
    return pl.pallas_call(
        lambda *refs: link_kernel(pairs, *refs),
        out_shape=[shape(dims, BF), shape(dims, F32)],
        in_specs=[SMEM, SMEM] + [VMEM] * 8,
        out_specs=[VMEM, VMEM],
        scratch_shapes=[pltpu.VMEM((16, n, n), F32)],
        compiler_params=PARAMS,
        name="link",
    )(ids, order, *w, *y)


def solve_kernel(pairs, ids_ref, order_ref, keep_ref, recv_ref, link_ref, far_ref, local_ref, out_ref, all_ref):
    piece = link_ref.shape[2]
    n = local_ref.shape[2]
    mine = ids_ref[3]
    for k in range(4):
        all_ref[pl.ds((mine ^ k) * piece, piece), :] = link_ref[k, 0]
        all_ref[pl.ds((mine ^ (k + 4)) * piece, piece), :] = far_ref[k, 0]
    coefs = []
    for s in range(4):
        a = order_ref[0, s]
        value = keep_ref[a] + recv_ref[a].astype(F32)
        for t in range(s):
            block = all_ref[pl.ds(pairs.index((t, s)) * n, n), :]
            value = value + jnp.dot(coefs[t], block, preferred_element_type=F32)
        coefs.append((value * local_ref[a]).astype(BF))
        out_ref[a] = coefs[s]


def solve(ids, order, keep, recv, link, far, local, pairs):
    n = keep.shape[2]
    return pl.pallas_call(
        lambda *refs: solve_kernel(pairs, *refs),
        out_shape=shape(keep.shape, BF),
        in_specs=[SMEM, SMEM] + [VMEM] * 5,
        out_specs=VMEM,
        scratch_shapes=[pltpu.VMEM((len(pairs) * n, n), BF)],
        compiler_params=PARAMS,
        name="solve",
    )(ids, order, keep, recv, link, far, local)


def most_kernel(ids_ref, x_ref, *refs):
    near_refs, far_ref, w_refs, out_ref = refs[:3], refs[3], refs[4:8], refs[8]
    rows = far_ref.shape[2]
    mine = ids_ref[3]
    for part in range(2):
        total = 0.0
        for a, w_ref in enumerate(w_refs):
            blocks = [near_refs[k][a] if part == 0 else far_ref[k, a] for k in range(3)]
            left = jnp.concatenate(blocks, axis=0)
            total = total + jnp.dot(left, w_ref[...], preferred_element_type=F32)
        for k in range(3):
            spot = pl.ds((mine ^ (k + 4 * part)) * rows, rows)
            out_ref[spot, :] = x_ref[spot, :] + total[k * rows : (k + 1) * rows, :]


def update_most(ids, state, near, far, w):
    cells, width = state.shape
    n = w[0].shape[0]
    step = 256
    tall = pl.BlockSpec((cells, step), lambda i: (0, i))
    whole = pl.BlockSpec(near[0].shape, lambda i: (0, 0, 0))
    whole_far = pl.BlockSpec(far.shape, lambda i: (0, 0, 0, 0))
    return pl.pallas_call(
        most_kernel,
        out_shape=shape((cells, width), F32),
        grid=(width // step,),
        in_specs=[SMEM, tall] + [whole] * 3 + [whole_far]
        + [pl.BlockSpec((n, step), lambda i: (0, i))] * 4,
        out_specs=tall,
        compiler_params=PARAMS,
        name="update_most",
    )(ids, state, *near, far, *w)


def rest_kernel(ids_ref, x_ref, near_ref, far_ref, w0_ref, w1_ref, w2_ref, w3_ref, _, out_ref):
    first = pl.program_id(0) == 0
    total = x_ref[...]
    for a, w_ref in enumerate((w0_ref, w1_ref, w2_ref, w3_ref)):
        left = jnp.where(first, near_ref[a], far_ref[a])
        total = total + jnp.dot(left, w_ref[...], preferred_element_type=F32)
    out_ref[...] = total


def update_rest(ids, state, near, far, w, most):
    cells, width = state.shape
    n = w[0].shape[0]
    rows = near.shape[1]
    block = pl.BlockSpec((rows, width), lambda i, ids: (ids[3] ^ (3 + 4 * i), 0))
    coef = pl.BlockSpec(near.shape, lambda i, ids: (0, 0, 0))
    wide = pl.BlockSpec((n, width), lambda i, ids: (0, 0))
    return pl.pallas_call(
        rest_kernel,
        out_shape=shape((cells, width), F32),
        grid_spec=pltpu.PrefetchScalarGridSpec(
            num_scalar_prefetch=1,
            grid=(2,),
            in_specs=[block, coef, coef] + [wide] * 4 + [pl.BlockSpec(memory_space=pl.ANY)],
            out_specs=block,
        ),
        input_output_aliases={8: 0},
        compiler_params=PARAMS,
        name="update_rest",
    )(ids, state, near, far, *w, most)


def spread_up(block):
    pair = jnp.stack([block, mem_swap(block, 4)])
    near = jnp.concatenate([pair, mem_swap(pair, 2)])
    return near, mem_swap(near, 1)


def on_device(state, obs_anom, innov, pattern, distance, taper, order):
    members = lax.axis_size("mem") * state.shape[1]
    scale = 1.0 / (members - 1)
    num_obs = obs_anom.shape[0]
    arrivals = order.shape[1]
    mem = lax.axis_index("mem")
    core, low, high = mem % 2, mem // 2 % 2, mem // 4
    mine = core * 4 + low * 2 + high
    ids = jnp.stack([core, low, high, mine]).astype(jnp.int32)
    pairs = [(t, s) for t in range(arrivals) for s in range(t + 1, arrivals)]

    y_one = send_one(obs_anom)
    y_two = send_two(y_one)
    half, other = sum_gram(dot_t(obs_anom, obs_anom), core)
    y_three = send_three(after(obs_anom, half))
    weights = weigh(ids, half, other, innov, scale)
    w_three = send_three(weights)
    w_one = send_one(after(weights, y_one))
    w_two = send_two(after(w_one, y_two))
    y_wraps = send_wraps(after(y_three, weights))
    y = [obs_anom, *pick_batches(y_one, y_two, *y_wraps), y_three]
    give, keep = cross_halves(ids, state, y)
    w_three = after(w_three, w_one, w_two)
    one_wrap, two_wrap = send_wraps(w_three)
    give, keep = halve(1, ids, keep, mem_swap(after(give, w_three), 1))
    w_wraps = after(one_wrap, give), after(two_wrap, give)
    w = [weights, *pick_batches(w_one, w_two, *w_wraps), w_three]
    give, keep = halve(2, ids, keep, mem_swap(give, 2))
    cross_recv = mem_swap(give, 4)

    link_give, link_keep = link_halves(ids, order, w, y, pairs)
    link_give, link_keep = halve(1, ids, link_keep, after(mem_swap(link_give, 1), give))
    link_recv = after(mem_swap(link_give, 2), cross_recv)
    link_give, link_keep = halve(2, ids, link_keep, link_recv)
    link = (link_keep + mem_swap(link_give, 4).astype(F32)).astype(BF)
    link_near, link_far = spread_up(link)

    onehot = (distance[0][..., None] == jnp.arange(taper.shape[0], dtype=jnp.int32)).astype(F32)
    local = pattern[0].astype(F32) * jnp.sum(onehot * taper, axis=-1)
    local = lax.dynamic_index_in_dim(local, mine, 1, keepdims=False) * scale
    local = jnp.repeat(local, num_obs // local.shape[1], axis=1)[:, None, :]
    coefs = solve(ids, order, keep, cross_recv, link_near, link_far, local, pairs)
    high_c = mem_swap(coefs, 4)
    low_c = mem_swap(coefs, 2)
    both_c = mem_swap(high_c, 2)
    far_most = mem_swap(jnp.stack([coefs, high_c, low_c]), 1)
    most = update_most(ids, state, [coefs, high_c, low_c], far_most, w)
    far_rest = mem_swap(after(both_c, most), 1)
    return update_rest(ids, state, both_c, far_rest, w, most)


def solution(mesh):
    return jax.shard_map(
        on_device,
        mesh=mesh,
        in_specs=(
            P("band", "mem"),
            P("band", "mem"),
            P("band", "mem"),
            P("band", None, None, None),
            P("band", None, None, None),
            P(),
            P("band", None),
        ),
        out_specs=P("band", "mem"),
        check_vma=False,
    )
```

```python
import jax
import jax.numpy as jnp
from jax import lax
from jax.experimental import pallas as pl
from jax.experimental.pallas import tpu as pltpu
from jax.sharding import PartitionSpec as P

HIGH = lax.Precision.HIGHEST
BF = jnp.bfloat16
F32 = jnp.float32
RING = 4
VMEM = pl.BlockSpec(memory_space=pltpu.VMEM)
SMEM = pl.BlockSpec(memory_space=pltpu.SMEM)
PARAMS = pltpu.CompilerParams(vmem_limit_bytes=48 * 2**20)


def shape(dims, dtype):
    return jax.ShapeDtypeStruct(dims, dtype)


def mem_swap(value, bit):
    count = lax.axis_size("mem")
    return lax.ppermute(value, "mem", [(m, m ^ bit) for m in range(count)])


def band_send(value, pairs):
    return lax.ppermute(value, "band", pairs)


def after(value, *deps):
    return lax.optimization_barrier((value,) + deps)[0]


def send_three(own):
    bands = lax.axis_size("band")
    return band_send(own, [(s, (s + 3) % bands) for s in range(bands)])


def send_one(own):
    bands = lax.axis_size("band")
    return band_send(own, [(s, s + 1) for s in range(bands) if s % RING < 3])


def send_two(one):
    bands = lax.axis_size("band")
    return band_send(one, [(s, s + 1) for s in range(bands) if s % RING in (1, 2)])


def send_wraps(three):
    bands = lax.axis_size("band")
    two = band_send(three, [(s, s - 1) for s in range(bands) if s % RING in (1, 2)])
    one = band_send(three, [(s, s - 2) for s in range(bands) if s % RING == 2])
    return one, two


def pick_batches(one, two, one_wrap, two_wrap):
    y = lax.axis_index("band") % RING
    return [jnp.where(y < 1, one_wrap, one), jnp.where(y < 2, two_wrap, two)]


def dot_t(a, b):
    return lax.dot_general(a, b, (((1,), (1,)), ((), ())), preferred_element_type=F32)


def sum_gram(part, core):
    rows = part.shape[0] // 2
    halves = part.reshape(2, rows, part.shape[1])
    keep = lax.dynamic_index_in_dim(halves, core, 0, keepdims=False)
    give = lax.dynamic_index_in_dim(halves, 1 - core, 0, keepdims=False)
    half = keep + mem_swap(give, 1)
    half = half + mem_swap(half, 2)
    half = half + mem_swap(half, 4)
    return half, mem_swap(half, 1)


def split(x):
    top = x.astype(BF)
    return top, (x - top.astype(F32)).astype(BF)


def dot_split(a, b):
    (a_top, a_low), (b_top, b_low) = a, b
    small = jnp.dot(a_top, b_low, preferred_element_type=F32)
    small = small + jnp.dot(a_low, b_top, preferred_element_type=F32)
    return small + jnp.dot(a_top, b_top, preferred_element_type=F32)


def dot_high(a, b):
    return jnp.dot(a, b, precision=HIGH, preferred_element_type=F32)


def weigh_kernel(scale, ids_ref, half_ref, other_ref, innov_ref, out_ref, x_ref, a_ref):
    rows, n = half_ref.shape
    core = ids_ref[0]
    i = lax.broadcasted_iota(jnp.int32, (n, n), 0)
    j = lax.broadcasted_iota(jnp.int32, (n, n), 1)
    eye = jnp.where(i == j, 1.0, 0.0).astype(F32)
    a_ref[pl.ds(core * rows, rows), :] = half_ref[...] * scale
    a_ref[pl.ds((1 - core) * rows, rows), :] = other_ref[...] * scale
    a = a_ref[...] + eye
    a_ref[...] = a
    most = jnp.max(jnp.sum(jnp.abs(a), axis=1, keepdims=True)) * 1.0001
    rho = (most - 1.0) / (most + 1.0)
    square = rho * rho
    grow = 2.0 / (2.0 - square)
    start = 2.0 / (1.0 + most)
    x_ref[...] = (2.0 * eye - a * start) * (start * grow)
    rho = square / (2.0 - square)

    def improve(product, rho):
        square = rho * rho
        grow = 2.0 / (2.0 - square)
        x = x_ref[...]
        r = eye - product(a_ref[...], x)
        x_ref[...] = (x + product(x, r)) * grow
        return square / (2.0 - square)

    @pl.when(most < 200.0)
    def _():
        a_parts = split(a_ref[...])

        def improve_fast(rho):
            square = rho * rho
            grow = 2.0 / (2.0 - square)
            x = x_ref[...]
            r = eye - dot_split(a_parts, split(x))
            step = jnp.dot(x.astype(BF), r.astype(BF), preferred_element_type=F32)
            x_ref[...] = (x + step) * grow
            return square / (2.0 - square)

        lax.while_loop(lambda rho: rho > 5e-3, improve_fast, rho)

    @pl.when(most >= 200.0)
    def _():
        lax.while_loop(lambda rho: rho > 5e-3, lambda rho: improve(dot_high, rho), rho)

    x = x_ref[...]
    r = eye - dot_high(a_ref[...], x)
    x = x + jnp.dot(x.astype(BF), r.astype(BF), preferred_element_type=F32)
    out_ref[...] = dot_split(split(x), split(innov_ref[...])).astype(BF)


def weigh(ids, half, other, innov, scale):
    n, width = innov.shape
    return pl.pallas_call(
        lambda *refs: weigh_kernel(scale, *refs),
        out_shape=shape((n, width), BF),
        in_specs=[SMEM, VMEM, VMEM, VMEM],
        out_specs=VMEM,
        scratch_shapes=[pltpu.VMEM((n, n), F32)] * 2,
        compiler_params=PARAMS,
        name="weigh",
    )(ids, half, other, innov)


def cross_kernel(ids_ref, x_ref, y0_ref, y1_ref, y2_ref, y3_ref, give_ref, keep_ref):
    rows = give_ref.shape[1]
    core = ids_ref[0]
    x = x_ref[pl.ds((1 - core) * rows, rows), :].astype(BF)
    for a, y_ref in enumerate((y0_ref, y1_ref, y2_ref, y3_ref)):
        give_ref[a] = dot_t(x, y_ref[...]).astype(BF)
    x = x_ref[pl.ds(core * rows, rows), :].astype(BF)
    for a, y_ref in enumerate((y0_ref, y1_ref, y2_ref, y3_ref)):
        keep_ref[a] = dot_t(x, y_ref[...])


def cross_halves(ids, state, y):
    rows = state.shape[0] // 2
    num_obs = y[0].shape[0]
    return pl.pallas_call(
        cross_kernel,
        out_shape=[shape((4, rows, num_obs), BF), shape((4, rows, num_obs), F32)],
        in_specs=[SMEM] + [VMEM] * 5,
        out_specs=[VMEM, VMEM],
        compiler_params=PARAMS,
        name="cross",
    )(ids, state, *y)


def halve_kernel(bit, ids_ref, keep_ref, recv_ref, give_ref, out_ref):
    rows = give_ref.shape[1]
    own = pl.ds(ids_ref[bit] * rows, rows)
    far = pl.ds((1 - ids_ref[bit]) * rows, rows)
    give_ref[...] = (keep_ref[:, far, :] + recv_ref[:, far, :].astype(F32)).astype(BF)
    out_ref[...] = keep_ref[:, own, :] + recv_ref[:, own, :].astype(F32)


def halve(bit, ids, keep, recv):
    a, rows, cols = keep.shape
    dims = (a, rows // 2, cols)
    return pl.pallas_call(
        lambda *refs: halve_kernel(bit, *refs),
        out_shape=[shape(dims, BF), shape(dims, F32)],
        in_specs=[SMEM, VMEM, VMEM],
        out_specs=[VMEM, VMEM],
        compiler_params=PARAMS,
        name="halve",
    )(ids, keep, recv)


def link_kernel(pairs, ids_ref, order_ref, *refs):
    w_refs, y_refs, (give_ref, keep_ref, all_ref) = refs[:4], refs[4:8], refs[8:]
    n = all_ref.shape[2]
    for t in range(4):
        for s in range(4):
            if s != t:
                all_ref[4 * t + s] = dot_t(w_refs[t][...], y_refs[s][...])
    core = ids_ref[0]
    half = len(pairs) // 2

    def pick(p):
        first = second = 0
        for k, (t, s) in enumerate(pairs):
            first = jnp.where(p == k, order_ref[0, t], first)
            second = jnp.where(p == k, order_ref[0, s], second)
        return all_ref[4 * first + second]

    for k in range(half):
        give_ref[0, pl.ds(k * n, n), :] = pick((1 - core) * half + k).astype(BF)
        keep_ref[0, pl.ds(k * n, n), :] = pick(core * half + k)


def link_halves(ids, order, w, y, pairs):
    n = y[0].shape[0]
    dims = (1, len(pairs) // 2 * n, n)
    return pl.pallas_call(
        lambda *refs: link_kernel(pairs, *refs),
        out_shape=[shape(dims, BF), shape(dims, F32)],
        in_specs=[SMEM, SMEM] + [VMEM] * 8,
        out_specs=[VMEM, VMEM],
        scratch_shapes=[pltpu.VMEM((16, n, n), F32)],
        compiler_params=PARAMS,
        name="link",
    )(ids, order, *w, *y)


def solve_kernel(pairs, ids_ref, order_ref, keep_ref, recv_ref, link_ref, far_ref, local_ref, out_ref, all_ref):
    piece = link_ref.shape[2]
    n = local_ref.shape[2]
    mine = ids_ref[3]
    for k in range(4):
        all_ref[pl.ds((mine ^ k) * piece, piece), :] = link_ref[k, 0]
        all_ref[pl.ds((mine ^ (k + 4)) * piece, piece), :] = far_ref[k, 0]
    coefs = []
    for s in range(4):
        a = order_ref[0, s]
        value = keep_ref[a] + recv_ref[a].astype(F32)
        for t in range(s):
            block = all_ref[pl.ds(pairs.index((t, s)) * n, n), :]
            value = value + jnp.dot(coefs[t], block, preferred_element_type=F32)
        coefs.append((value * local_ref[a]).astype(BF))
        out_ref[a] = coefs[s]


def solve(ids, order, keep, recv, link, far, local, pairs):
    n = keep.shape[2]
    return pl.pallas_call(
        lambda *refs: solve_kernel(pairs, *refs),
        out_shape=shape(keep.shape, BF),
        in_specs=[SMEM, SMEM] + [VMEM] * 5,
        out_specs=VMEM,
        scratch_shapes=[pltpu.VMEM((len(pairs) * n, n), BF)],
        compiler_params=PARAMS,
        name="solve",
    )(ids, order, keep, recv, link, far, local)


def most_kernel(ids_ref, x_ref, *refs):
    near_refs, far_ref, w_refs, out_ref = refs[:3], refs[3], refs[4:8], refs[8]
    rows = far_ref.shape[2]
    mine = ids_ref[3]
    for part in range(2):
        total = 0.0
        for a, w_ref in enumerate(w_refs):
            blocks = [near_refs[k][a] if part == 0 else far_ref[k, a] for k in range(3)]
            left = jnp.concatenate(blocks, axis=0)
            total = total + jnp.dot(left, w_ref[...], preferred_element_type=F32)
        for k in range(3):
            spot = pl.ds((mine ^ (k + 4 * part)) * rows, rows)
            out_ref[spot, :] = x_ref[spot, :] + total[k * rows : (k + 1) * rows, :]


def update_most(ids, state, near, far, w):
    cells, width = state.shape
    n = w[0].shape[0]
    step = 256
    tall = pl.BlockSpec((cells, step), lambda i: (0, i))
    whole = pl.BlockSpec(near[0].shape, lambda i: (0, 0, 0))
    whole_far = pl.BlockSpec(far.shape, lambda i: (0, 0, 0, 0))
    return pl.pallas_call(
        most_kernel,
        out_shape=shape((cells, width), F32),
        grid=(width // step,),
        in_specs=[SMEM, tall] + [whole] * 3 + [whole_far]
        + [pl.BlockSpec((n, step), lambda i: (0, i))] * 4,
        out_specs=tall,
        compiler_params=PARAMS,
        name="update_most",
    )(ids, state, *near, far, *w)


def rest_kernel(ids_ref, x_ref, near_ref, far_ref, w0_ref, w1_ref, w2_ref, w3_ref, _, out_ref):
    first = pl.program_id(0) == 0
    total = x_ref[...]
    for a, w_ref in enumerate((w0_ref, w1_ref, w2_ref, w3_ref)):
        left = jnp.where(first, near_ref[a], far_ref[a])
        total = total + jnp.dot(left, w_ref[...], preferred_element_type=F32)
    out_ref[...] = total


def update_rest(ids, state, near, far, w, most):
    cells, width = state.shape
    n = w[0].shape[0]
    rows = near.shape[1]
    block = pl.BlockSpec((rows, width), lambda i, ids: (ids[3] ^ (3 + 4 * i), 0))
    coef = pl.BlockSpec(near.shape, lambda i, ids: (0, 0, 0))
    wide = pl.BlockSpec((n, width), lambda i, ids: (0, 0))
    return pl.pallas_call(
        rest_kernel,
        out_shape=shape((cells, width), F32),
        grid_spec=pltpu.PrefetchScalarGridSpec(
            num_scalar_prefetch=1,
            grid=(2,),
            in_specs=[block, coef, coef] + [wide] * 4 + [pl.BlockSpec(memory_space=pl.ANY)],
            out_specs=block,
        ),
        input_output_aliases={8: 0},
        compiler_params=PARAMS,
        name="update_rest",
    )(ids, state, near, far, *w, most)


def spread_up(block):
    pair = jnp.stack([block, mem_swap(block, 4)])
    near = jnp.concatenate([pair, mem_swap(pair, 2)])
    return near, mem_swap(near, 1)


def on_device(state, obs_anom, innov, pattern, distance, taper, order):
    members = lax.axis_size("mem") * state.shape[1]
    scale = 1.0 / (members - 1)
    num_obs = obs_anom.shape[0]
    arrivals = order.shape[1]
    mem = lax.axis_index("mem")
    core, low, high = mem % 2, mem // 2 % 2, mem // 4
    mine = core * 4 + low * 2 + high
    ids = jnp.stack([core, low, high, mine]).astype(jnp.int32)
    pairs = [(t, s) for t in range(arrivals) for s in range(t + 1, arrivals)]

    y_one = send_one(obs_anom)
    y_two = send_two(y_one)
    half, other = sum_gram(dot_t(obs_anom, obs_anom), core)
    y_three = send_three(after(obs_anom, half))
    weights = weigh(ids, half, other, innov, scale)
    w_three = send_three(weights)
    w_one = send_one(after(weights, y_one))
    w_two = send_two(after(w_one, y_two))
    y_wraps = send_wraps(after(y_three, weights))
    y = [obs_anom, *pick_batches(y_one, y_two, *y_wraps), y_three]
    give, keep = cross_halves(ids, state, y)
    w_three = after(w_three, w_one, w_two)
    one_wrap, two_wrap = send_wraps(w_three)
    give, keep = halve(1, ids, keep, mem_swap(after(give, w_three), 1))
    w_wraps = after(one_wrap, give), after(two_wrap, give)
    w = [weights, *pick_batches(w_one, w_two, *w_wraps), w_three]
    give, keep = halve(2, ids, keep, mem_swap(give, 2))
    cross_recv = mem_swap(give, 4)

    link_give, link_keep = link_halves(ids, order, w, y, pairs)
    link_give, link_keep = halve(1, ids, link_keep, after(mem_swap(link_give, 1), give))
    link_give, link_keep = halve(2, ids, link_keep, mem_swap(link_give, 2))
    link_recv = after(mem_swap(link_give, 4), cross_recv)
    link = (link_keep + link_recv.astype(F32)).astype(BF)
    link_near, link_far = spread_up(link)

    onehot = (distance[0][..., None] == jnp.arange(taper.shape[0], dtype=jnp.int32)).astype(F32)
    local = pattern[0].astype(F32) * jnp.sum(onehot * taper, axis=-1)
    local = lax.dynamic_index_in_dim(local, mine, 1, keepdims=False) * scale
    local = jnp.repeat(local, num_obs // local.shape[1], axis=1)[:, None, :]
    coefs = solve(ids, order, keep, cross_recv, link_near, link_far, local, pairs)
    high_c = mem_swap(coefs, 4)
    low_c = mem_swap(coefs, 2)
    both_c = mem_swap(high_c, 2)
    far_most = mem_swap(jnp.stack([coefs, high_c, low_c]), 1)
    most = update_most(ids, state, [coefs, high_c, low_c], far_most, w)
    far_rest = mem_swap(after(both_c, most), 1)
    return update_rest(ids, state, both_c, far_rest, w, most)


def solution(mesh):
    return jax.shard_map(
        on_device,
        mesh=mesh,
        in_specs=(
            P("band", "mem"),
            P("band", "mem"),
            P("band", "mem"),
            P("band", None, None, None),
            P("band", None, None, None),
            P(),
            P("band", None),
        ),
        out_specs=P("band", "mem"),
        check_vma=False,
    )
```
